32 devices in a mesh: dp: 8 (over z, core), fsdp: 4 (over y, x).
Axes of the slice: x: 2, y: 2, z: 4, core: 2. Of those that a mesh axis runs over, the one named last changes fastest.
Arguments:
- tokens: bfloat16 [64, 256, 1024], P(('dp', 'fsdp')), may hold values from -6 to 6
- encoded: bfloat16 [64, 512, 1024], P(('dp', 'fsdp')), may hold values from -6 to 6
- cotangent: bfloat16 [64, 256, 1024], P(('dp', 'fsdp')), may hold values from -6 to 6
- lengths: int32 [64], replicated, may hold values from 32 to 256, as said below
- enc_segments: int32 [64, 512], replicated, may hold values from 0 to 3, never falling along the last dimension, each value on 1 to 256 neighbouring positions
- placement: int32 [64], replicated, may hold values from 0 to 63, as said below
- buckets: int32 [256], replicated, may hold values from 0 to 31, as said below
- self_query: bfloat16 [1024, 1024], P(('dp', 'fsdp')), may hold values from -0.1875 to 0.1875
- self_keyval: bfloat16 [1024, 1024], P(('dp', 'fsdp')), may hold values from -0.1875 to 0.1875
- self_out: bfloat16 [1024, 1024], P(('dp', 'fsdp')), may hold values from -1.5 to 1.5
- cross_query: bfloat16 [1024, 1024], P(('dp', 'fsdp')), may hold values from -0.1875 to 0.1875
- cross_keyval: bfloat16 [1024, 1024], P(('dp', 'fsdp')), may hold values from -0.1875 to 0.1875
- cross_out: bfloat16 [1024, 1024], P(('dp', 'fsdp')), may hold values from -2 to 2
- feed_in: bfloat16 [1024, 5632], P(('dp', 'fsdp')), may hold values from -0.1875 to 0.1875
- feed_out: bfloat16 [2816, 1024], P(('dp', 'fsdp')), may hold values from -0.21875 to 0.21875
- norm_self: bfloat16 [1024], P(('dp', 'fsdp')), may hold values from 0.099609375 to 1.8984375
- norm_cross: bfloat16 [1024], P(('dp', 'fsdp')), may hold values from 0.099609375 to 1.8984375
- norm_feed: bfloat16 [1024], P(('dp', 'fsdp')), may hold values from 0.099609375 to 1.8984375
- bias_table: bfloat16 [512], P(('dp', 'fsdp')), may hold values from -4 to 4
Outputs:
- output: bfloat16 [64, 256, 1024], P(('dp', 'fsdp'))
- grad_tokens: float32 [64, 256, 1024], P(('dp', 'fsdp'))
- grad_encoded: float32 [64, 512, 1024], P(('dp', 'fsdp'))
- grad_self_query: float32 [1024, 1024], P(('dp', 'fsdp'))
- grad_self_keyval: float32 [1024, 1024], P(('dp', 'fsdp'))
- grad_self_out: float32 [1024, 1024], P(('dp', 'fsdp'))
- grad_cross_query: float32 [1024, 1024], P(('dp', 'fsdp'))
- grad_cross_keyval: float32 [1024, 1024], P(('dp', 'fsdp'))
- grad_cross_out: float32 [1024, 1024], P(('dp', 'fsdp'))
- grad_feed_in: float32 [1024, 5632], P(('dp', 'fsdp'))
- grad_feed_out: float32 [2816, 1024], P(('dp', 'fsdp'))
- grad_norm_self: float32 [1024], P(('dp', 'fsdp'))
- grad_norm_cross: float32 [1024], P(('dp', 'fsdp'))
- grad_norm_feed: float32 [1024], P(('dp', 'fsdp'))
- grad_bias_table: float32 [512], P(('dp', 'fsdp'))
The draws below stay inside these ranges and needn't reach their ends.
Inputs may be any that keep to these rules, and one draw needn't show every extreme that they name: `lengths`: one sequence has exactly 256 tokens. `enc_segments`: nondecreasing along each row; every id occurs in each row. A permutation; each sequence stays in its block of 8: placement[k] // 8 equals k // 8. `buckets`: nondecreasing in the distance, 0 at distance 0, every bucket used.
All inputs are finite; a program needn't handle non-finite values.
Results may differ from the reference program's by a relative error of at most 0.023.
Values may be sent and summed in bfloat16 or wider, within the bound.
No kernel may reach another device: no remote copies, remote signals or barrier semaphores. Data moves between devices by JAX's collectives and lax.ppermute only.
A program may use at most 320 MiB of HBM per device.

```python
import math
import jax
import jax.numpy as jnp
import numpy as np
from jax import lax

D = 1024
HEADS = 16
HEAD_DIM = 64
KV_HEADS = 8
FF = 2816
BUCKETS = 32
SEQ_LEN = 256
ENC = 512
ENC_SEGS = 4
SLOTS = 2
NSEQ = 64
GROUP = 8


def dealt_lengths(key):
    base_key, pick_key = jax.random.split(jax.random.fold_in(key, 11))
    values = jax.random.randint(base_key, (NSEQ,), SEQ_LEN // 8, SEQ_LEN + 1)
    chosen = jax.random.randint(pick_key, (), 0, NSEQ)
    return jnp.where(jnp.arange(NSEQ) == chosen, SEQ_LEN, values).astype(jnp.int32)


def draw_lengths(key, part):
    return dealt_lengths(key)


def draw_placement(key, part):
    lengths = dealt_lengths(key)
    group_count = NSEQ // GROUP
    width = GROUP // SLOTS
    grid = lengths.reshape(group_count, GROUP)
    spots = jnp.arange(GROUP, dtype=jnp.int32)
    score = grid * GROUP + spots[None, :]
    ranked = jnp.argsort(-score, axis=1).astype(jnp.int32)
    passes = spots // width
    within = spots % width
    device_in = jnp.where(passes % 2 == 0, within, width - 1 - within)
    slot_of_rank = (device_in * SLOTS + passes).astype(jnp.int32)
    base = (jnp.arange(group_count, dtype=jnp.int32) * GROUP)[:, None]
    order = jnp.zeros((group_count, GROUP), jnp.int32).at[:, slot_of_rank].set(ranked + base)
    return order.reshape(NSEQ).astype(jnp.int32)


def draw_buckets(key, part):
    shuffled = jax.random.permutation(key, SEQ_LEN - 1).astype(jnp.int32) + 1
    boundaries = shuffled[:BUCKETS - 1]
    places = jnp.arange(SEQ_LEN, dtype=jnp.int32)
    return jnp.sum((places[:, None] >= boundaries[None, :]).astype(jnp.int32), axis=1).astype(jnp.int32)


def spiked(values, own_key, source, target, shards_of, factor):
    owner, partner = [(jnp.arange(values.shape[dim]) // (values.shape[dim] // shards_of)).reshape([-1 if axis == dim else 1 for axis in range(values.ndim)]) for dim in (source, target)]
    chosen = jax.random.permutation(own_key, shards_of)[partner]
    strong = (owner == chosen) | (owner == (partner + shards_of // 2) % shards_of)
    return jnp.where(strong, factor * values, values)


def level_of(key, shape, shards, low, largest):
    factor_of = 1.0
    for position, parts in shards:
        draws = jax.random.uniform(jax.random.fold_in(jax.random.fold_in(key, 6), position), (parts,), jnp.float32, low / len(shards), largest / len(shards))
        factor_of = factor_of * jnp.repeat(jnp.exp(draws), shape[position] // parts).reshape((-1,) + (1,) * (len(shape) - 1 - position))
    return factor_of


def length_profile(amount, total, limit, skew):
    weights = [(1 << 20) // math.isqrt(standing ** skew) + 1 for standing in range(2, amount + 1)]
    surplus, holding = total - limit - (amount - 1), [1] * (amount - 1)
    while surplus > 0:
        free = [i for i in range(amount - 1) if holding[i] < limit]
        whole, remaining = sum([weights[i] for i in free]), surplus
        for i in free:
            addition = min(limit - holding[i], max(1, remaining * weights[i] // whole), surplus)
            holding[i] = holding[i] + addition
            surplus = surplus - addition
    return np.array([limit] + holding)


def uneven_parts(rng, count, total, most, slope):
    if count == 2:
        one = jax.random.randint(rng, (), max(1, total - most), min(most, total - 1) + 1)
        return jnp.stack([one, total - one])
    sizes = jnp.asarray(length_profile(count, total, most, slope), jnp.int32)
    pairs = (count - 1) // 2
    source_of, receiver = sizes[1:1 + 2 * pairs:2], sizes[2:2 + 2 * pairs:2]
    slack = jnp.minimum(source_of - 1, most - receiver)
    moved = jax.random.randint(jax.random.fold_in(rng, 1), (pairs,), 0, 1 << 20) % (slack + 1)
    sizes = sizes.at[1:1 + 2 * pairs:2].set(source_of - moved).at[2:2 + 2 * pairs:2].set(receiver + moved)
    return sizes[jax.random.permutation(jax.random.fold_in(rng, 2), count)]


def scatter_about(key, dims, scale, limit, cuts=(), kind=jnp.bfloat16):
    drawn = scale * jax.random.normal(key, dims, jnp.float32)
    if cuts:
        drawn = drawn * level_of(key, dims, cuts, -0.22, 0.18)
    return jnp.clip(drawn, -limit, limit).astype(kind)


def bell_draw_with(own_key, extent, scale, most, cuts, heavy, kind=jnp.bfloat16):
    values = scale * jax.random.normal(own_key, extent, jnp.float32)
    if cuts:
        values = values * level_of(own_key, extent, cuts, -0.22, 0.18)
    return jnp.clip(spiked(values, jax.random.fold_in(own_key, 3), *heavy), -most, most).astype(kind)


def setup_inputs(seed: int = 0) -> dict:
    seeds = jax.random.split(jax.random.key(seed), 20)
    return {
        "tokens": bell_draw_with(seeds[0], (NSEQ, SEQ_LEN, D), 1.0, 6.0, ((0, 32),), (0, 2, 32, 2.75)),
        "encoded": scatter_about(seeds[1], (NSEQ, ENC, D), 1.0, 6.0, ((0, 32),)),
        "cotangent": scatter_about(seeds[2], (NSEQ, SEQ_LEN, D), 1.0, 6.0, ((0, 32),)),
        "lengths": draw_lengths(jax.random.fold_in(seeds[19], 71), 0),
        "enc_segments": jax.vmap(lambda own: jnp.searchsorted(jnp.cumsum(uneven_parts(own, ENC_SEGS, ENC, ENC // 2, 0)), jnp.arange(ENC), side="right"))(jax.random.split(seeds[4], NSEQ)).reshape((NSEQ, ENC)).astype(jnp.int32),
        "placement": draw_placement(jax.random.fold_in(seeds[19], 71), 0),
        "buckets": draw_buckets(jax.random.fold_in(seeds[19], 71), 0),
        "self_query": scatter_about(seeds[7], (D, HEADS * HEAD_DIM), D ** -0.5, 0.1875, ((0, 32),)),
        "self_keyval": scatter_about(seeds[8], (D, 2 * KV_HEADS * HEAD_DIM), D ** -0.5, 0.1875, ((0, 32),)),
        "self_out": scatter_about(seeds[9], (HEADS * HEAD_DIM, D), (max(1, D // 64)) ** -0.5, 1.5, ((0, 32),)),
        "cross_query": scatter_about(seeds[10], (D, HEADS * HEAD_DIM), D ** -0.5, 0.1875, ((0, 32),)),
        "cross_keyval": scatter_about(seeds[11], (D, 2 * KV_HEADS * HEAD_DIM), D ** -0.5, 0.1875, ((0, 32),)),
        "cross_out": scatter_about(seeds[12], (HEADS * HEAD_DIM, D), (max(1, D // 128)) ** -0.5, 2.0, ((0, 32),)),
        "feed_in": scatter_about(seeds[13], (D, 2 * FF), D ** -0.5, 0.1875, ((0, 32),)),
        "feed_out": scatter_about(seeds[14], (FF, D), (FF // 4) ** -0.5, 0.21875, ((0, 32),)),
        "norm_self": jnp.clip(1.0 + 0.18 * jax.random.normal(seeds[15], (D,), jnp.float32), 0.099609375, 1.8984375).astype(jnp.bfloat16),
        "norm_cross": jnp.clip(1.0 + 0.18 * jax.random.normal(seeds[16], (D,), jnp.float32), 0.099609375, 1.8984375).astype(jnp.bfloat16),
        "norm_feed": jnp.clip(1.0 + 0.18 * jax.random.normal(seeds[17], (D,), jnp.float32), 0.099609375, 1.8984375).astype(jnp.bfloat16),
        "bias_table": scatter_about(seeds[18], (BUCKETS * HEADS,), 1.0, 4.0, ((0, 32),)),
    }


@jax.custom_vjp
def low(v):
    return lax.optimization_barrier(v.astype(jnp.bfloat16)).astype(jnp.float32)

@jax.custom_vjp
def low_back(v):
    return v

def low_keep(v):
    return (low(v), None)

def low_pass(kept, grad):
    return (grad,)

def back_keep(v):
    return (v, None)

def back_low(kept, grad):
    return (low(grad),)
low.defvjp(low_keep, low_pass)
low_back.defvjp(back_keep, back_low)
EPSILON = 1e-06
NEGATIVE = -1e+30
PRECISE = lax.Precision.HIGHEST

def matmul(left_op, right_op):
    return jnp.dot(left_op, right_op, precision=PRECISE)

def rms_scale(values, gain_vec):
    return values * lax.rsqrt(lax.optimization_barrier(jnp.mean(values * values, axis=-1, keepdims=True)) + EPSILON) * gain_vec

def attend(queries, keyvals, rel_bias, allowed):
    row_count = queries.shape[0]
    key_count = keyvals.shape[0]
    groups = HEADS // KV_HEADS
    kv_width = KV_HEADS * HEAD_DIM
    factor = 1.0 / math.sqrt(HEAD_DIM)
    query_heads = queries.reshape(row_count, KV_HEADS, groups, HEAD_DIM)
    key_heads = keyvals[:, :kv_width].reshape(key_count, KV_HEADS, HEAD_DIM)
    value_heads = keyvals[:, kv_width:].reshape(key_count, KV_HEADS, HEAD_DIM)
    raw_scores = jnp.einsum('ikgd,jkd->kgij', query_heads, key_heads, precision=PRECISE) * factor + rel_bias
    scores = jnp.where(allowed, low_back(raw_scores), NEGATIVE)
    probs_soft = jax.nn.softmax(scores, axis=-1)
    mixed_heads = jnp.einsum('kgij,jkd->ikgd', low(probs_soft), value_heads, precision=PRECISE)
    return low(low_back(mixed_heads.reshape(row_count, HEADS * HEAD_DIM)))

def decoder_layer(tokens_row, encoded_row, length, segments_row, params, distance_bucket):
    self_query, self_keyval, self_out, cross_query, cross_keyval, cross_out, feed_in, feed_out, norm_self, norm_cross, norm_feed, bias_table = params
    groups = HEADS // KV_HEADS
    places = jnp.arange(SEQ_LEN, dtype=jnp.int32)
    is_valid = places < length
    self_allowed = (places[None, :] <= places[:, None]) & is_valid[None, :]
    seg_reach = places * ENC_SEGS // length
    cross_allowed = segments_row[None, :] <= seg_reach[:, None]
    table_grid = bias_table.reshape(BUCKETS, HEADS)
    rel_bias = jnp.transpose(table_grid[distance_bucket], (2, 0, 1)).reshape(KV_HEADS, groups, SEQ_LEN, SEQ_LEN)
    normed = low(rms_scale(tokens_row, norm_self))
    queries = low(low_back(matmul(normed, self_query)))
    keyvals = low(low_back(matmul(normed, self_keyval)))
    hidden_one = tokens_row + low_back(matmul(attend(queries, keyvals, rel_bias, self_allowed), self_out))
    normed = low(rms_scale(hidden_one, norm_cross))
    queries = low(low_back(matmul(normed, cross_query)))
    keyvals = low(low_back(matmul(encoded_row, cross_keyval)))
    hidden_two = hidden_one + low_back(matmul(attend(queries, keyvals, 0.0, cross_allowed), cross_out))
    normed = low(rms_scale(hidden_two, norm_feed))
    gate_up = low_back(matmul(normed, feed_in))
    inner_act = low(jax.nn.gelu(gate_up[:, :FF], approximate=True) * gate_up[:, FF:])
    result = hidden_two + low_back(matmul(inner_act, feed_out))
    return jnp.where(is_valid[:, None], result, 0.0)

def run_all(params, tokens_all, encoded_all, lengths, enc_segments, distance_bucket):
    group_size = math.gcd(NSEQ, max(1, 4096 // SEQ_LEN))
    blocks = NSEQ // group_size

    def per_sequence(tokens_row, encoded_row, length, segments_row):
        return decoder_layer(tokens_row, encoded_row, length, segments_row, params, distance_bucket)

    def scan_step(carry, block_item):
        token_block, encoded_block, length_block, segment_block = block_item
        return (carry, jax.vmap(per_sequence)(token_block, encoded_block, length_block, segment_block))
    stacked = (tokens_all.reshape(blocks, group_size, SEQ_LEN, D), encoded_all.reshape(blocks, group_size, ENC, D), lengths.reshape(blocks, group_size), enc_segments.reshape(blocks, group_size, ENC))
    carry, outputs = lax.scan(jax.checkpoint(scan_step), jnp.float32(0.0), stacked)
    return outputs.reshape(NSEQ, SEQ_LEN, D)

def reference(tokens, encoded, cotangent, lengths, enc_segments, placement, buckets, self_query, self_keyval, self_out, cross_query, cross_keyval, cross_out, feed_in, feed_out, norm_self, norm_cross, norm_feed, bias_table):
    places = jnp.arange(SEQ_LEN, dtype=jnp.int32)
    distance = jnp.clip(places[:, None] - places[None, :], 0, SEQ_LEN - 1).astype(jnp.int32)
    distance_bucket = buckets[distance]
    inverse = jnp.zeros((NSEQ,), jnp.int32).at[placement].set(jnp.arange(NSEQ, dtype=jnp.int32))
    given_cotangent = cotangent.astype(jnp.float32)[inverse]
    params = tuple((matrix.astype(jnp.float32) for matrix in (self_query, self_keyval, self_out, cross_query, cross_keyval, cross_out, feed_in, feed_out, norm_self, norm_cross, norm_feed, bias_table)))

    def whole(param_set, token_set, encoded_set):
        return run_all(param_set, token_set, encoded_set, lengths, enc_segments, distance_bucket)
    result, pullback = jax.vjp(whole, params, tokens.astype(jnp.float32), encoded.astype(jnp.float32))
    grad_params, grad_tokens, grad_encoded = pullback(given_cotangent)
    return (result.astype(jnp.bfloat16), grad_tokens, grad_encoded, grad_params[0], grad_params[1], grad_params[2], grad_params[3], grad_params[4], grad_params[5], grad_params[6], grad_params[7], grad_params[8], grad_params[9], grad_params[10], grad_params[11])
```

```python
import math

import jax
import jax.numpy as jnp
from jax import lax
from jax.experimental import pallas as pl
from jax.experimental.pallas import tpu as pltpu
from jax.sharding import PartitionSpec as P

HEADS = 16
HEAD_DIM = 64
KV_HEADS = 8
FF = 2816
BUCKETS = 32
ENC_SEGS = 4

EPSILON = 1e-06
NEGATIVE = -1e30
AXES = ("dp", "fsdp")
BF16 = jnp.bfloat16
F32 = jnp.float32
SMALL = 128


def matmul(left_op, right_op):
    return jnp.dot(left_op, right_op, preferred_element_type=F32)


def matmul_tn(left_op, right_op):
    return lax.dot_general(left_op, right_op, (((0,), (0,)), ((), ())), preferred_element_type=F32)


def matmul_nt(left_op, right_op):
    return lax.dot_general(left_op, right_op, (((1,), (1,)), ((), ())), preferred_element_type=F32)


class Grid:
    def __init__(self):
        self.planes = lax.axis_size("fsdp")
        self.lines = lax.axis_size("dp") // 2
        dp = lax.axis_index("dp")
        self.line, self.core, self.plane = dp // 2, dp % 2, lax.axis_index("fsdp")

    def send(self, array, line=0, core=0, plane=0):
        pairs = []
        for source in range(2 * self.lines * self.planes):
            z, c, s = source // (2 * self.planes), source // self.planes % 2, source % self.planes
            pairs.append((source, ((z ^ line) * 2 + (c ^ core)) * self.planes + (s ^ plane)))
        return lax.ppermute(array, AXES, pairs)


def place(shape, dtype, pieces, index, name):
    arrays, jobs = [], []
    for array, where in pieces:
        jobs.append((len(arrays), where))
        arrays.append(array)

    def body(index_ref, *refs):
        ins, out, sems = refs[: len(arrays)], refs[len(arrays)], refs[len(arrays) + 1]
        copies = [
            pltpu.make_async_copy(ins[i], out.at[where(index_ref)], sems.at[k])
            for k, (i, where) in enumerate(jobs)
        ]
        for copy in copies:
            copy.start()
        for copy in copies:
            copy.wait()

    return pl.pallas_call(
        body,
        out_shape=jax.ShapeDtypeStruct(shape, dtype),
        grid_spec=pltpu.PrefetchScalarGridSpec(
            num_scalar_prefetch=1,
            grid=(),
            in_specs=[pl.BlockSpec(memory_space=pl.ANY)] * len(arrays),
            out_specs=pl.BlockSpec(memory_space=pl.ANY),
            scratch_shapes=[pltpu.SemaphoreType.DMA((len(jobs),))],
        ),
        name=name,
    )(index, *arrays)


def spread(grid, block):
    if grid.planes != 4:
        return [(0, None, block)] + [
            (j, None, grid.send(block, plane=j)) for j in range(1, grid.planes)
        ]
    half = block.shape[0] // 2
    by_x = grid.send(block, plane=1)
    by_y = grid.send(block, plane=2)
    low = grid.send(by_x[:half], plane=2)
    high = grid.send(by_y[half:], plane=1)
    return [(0, None, block), (1, None, by_x), (2, None, by_y), (3, 0, low), (3, 1, high)]


def gather_rows(grid, index, shard, widths, name):
    rows, width = shard.shape
    lines, planes = grid.lines, grid.planes
    parts = [shard] + [grid.send(shard, line=j) for j in range(1, lines)]
    block = place(
        (lines, rows, width),
        shard.dtype,
        [(part, lambda ref, j=j: (ref[0] ^ j,)) for j, part in enumerate(parts)],
        index,
        name + "_line",
    )
    pieces = spread(grid, block)
    both = [(0, *piece) for piece in pieces] + [
        (1, j, part, grid.send(array, core=1)) for j, part, array in pieces
    ]
    half = lines // 2
    shape = (lines, 2, planes, rows)
    offset, outs, jobs = 0, [], []
    for w in widths:
        outs.append(jax.ShapeDtypeStruct((*shape, w), shard.dtype))
        for source, (c, j, part, _) in enumerate(both):
            span = pl.ds(0, lines) if part is None else pl.ds(part * half, half)
            jobs.append((source, len(outs) - 1, pl.ds(offset, w), span, c, j))
        offset += w
    n_in, n_out = len(both), len(outs)

    def body(index_ref, *refs):
        ins, dst, sems = refs[:n_in], refs[n_in : n_in + n_out], refs[n_in + n_out]
        copies = []
        for k, (source, out, columns, span, c, j) in enumerate(jobs):
            here = ins[source] if n_out == 1 else ins[source].at[:, :, columns]
            there = dst[out].at[span, index_ref[1] ^ c, index_ref[2] ^ j]
            copies.append(pltpu.make_async_copy(here, there, sems.at[k]))
        for copy in copies:
            copy.start()
        for copy in copies:
            copy.wait()

    whole = pl.pallas_call(
        body,
        out_shape=outs,
        grid_spec=pltpu.PrefetchScalarGridSpec(
            num_scalar_prefetch=1,
            grid=(),
            in_specs=[pl.BlockSpec(memory_space=pl.ANY)] * n_in,
            out_specs=[pl.BlockSpec(memory_space=pl.ANY)] * n_out,
            scratch_shapes=[pltpu.SemaphoreType.DMA((len(jobs),))],
        ),
        name=name + "_whole",
    )(index, *[array for _, _, _, array in both])
    return [array.reshape(-1, array.shape[-1]) for array in whole]


def scatter_rows(grid, terms):
    lines, planes = grid.lines, grid.planes
    width = terms.shape[-1]
    terms = terms.reshape(lines, 2, planes, -1, width)

    def pick(array, at, axis):
        return lax.dynamic_index_in_dim(array, at, axis, keepdims=False)

    other = grid.send(pick(terms, 1 - grid.core, 1), core=1)
    mine = pick(terms, grid.core, 1)

    def block(j):
        at = grid.plane ^ j
        return pick(mine, at, 1).astype(F32) + pick(other, at, 1).astype(F32)

    if planes != 4:
        own = block(0)
        for j in range(1, planes):
            own = own + grid.send(block(j).astype(BF16), plane=j).astype(F32)
    else:
        half = lines // 2
        far = block(3).astype(BF16)
        low = grid.send(far[:half], plane=2).astype(F32)
        high = grid.send(far[half:], plane=1).astype(F32)
        by_x, by_y = block(1), block(2)
        by_x = jnp.concatenate([by_x[:half] + low, by_x[half:]]).astype(BF16)
        by_y = jnp.concatenate([by_y[:half], by_y[half:] + high]).astype(BF16)
        own = block(0) + grid.send(by_x, plane=1).astype(F32)
        own = own + grid.send(by_y, plane=2).astype(F32)
    own = own.astype(BF16)
    total = pick(own, grid.line, 0).astype(F32)
    for j in range(1, lines):
        total = total + grid.send(pick(own, grid.line ^ j, 0), line=j).astype(F32)
    return total


def fetch_dealt(grid, array, found):
    slots, rest = array.shape[0], array.shape[1:]
    pieces = spread(grid, array) if slots == 2 else [
        (j, None, grid.send(array, plane=j) if j else array) for j in range(grid.planes)
    ]
    half = slots // 2

    def body(index_ref, found_ref, *refs):
        ins, out, sems = refs[: len(pieces)], refs[len(pieces)], refs[len(pieces) + 1]
        for t in range(slots):
            k = found_ref[t]
            away, slot = (k // slots) ^ index_ref[2], k % slots
            for i, (j, part, _) in enumerate(pieces):
                if part is None:
                    hit, at = away == j, slot
                else:
                    hit, at = (away == j) & (slot // half == part), slot % half

                @pl.when(hit)
                def _(i=i, at=at):
                    pltpu.make_async_copy(ins[i].at[at], out.at[t], sems.at[t]).start()

        for t in range(slots):
            pltpu.make_async_copy(ins[0].at[0], out.at[t], sems.at[t]).wait()

    return pl.pallas_call(
        body,
        out_shape=jax.ShapeDtypeStruct(array.shape, array.dtype),
        grid_spec=pltpu.PrefetchScalarGridSpec(
            num_scalar_prefetch=2,
            grid=(),
            in_specs=[pl.BlockSpec(memory_space=pl.ANY)] * len(pieces),
            out_specs=pl.BlockSpec(memory_space=pl.ANY),
            scratch_shapes=[pltpu.SemaphoreType.DMA((slots,))],
        ),
        name="fetch_dealt",
    )(grid_index(grid), found, *[piece for _, _, piece in pieces])


def grid_index(grid):
    return jnp.stack([grid.line, grid.core, grid.plane]).astype(jnp.int32)


PAIRS = KV_HEADS // 2
GROUPS = HEADS // KV_HEADS
WIDE = 2 * GROUPS * HEAD_DIM
NARROW = 2 * HEAD_DIM


def mm(left, right, dims):
    return lax.dot_general(left, right, ((dims[:1], dims[1:]), ((), ())), preferred_element_type=F32)


def softmax_mix(q, k, v, heads, mask_of, probs_ref, out_ref):
    for h in range(heads):
        kv = h // GROUPS
        q_h = q[:, h * HEAD_DIM : (h + 1) * HEAD_DIM]
        k_h = k[:, kv * HEAD_DIM : (kv + 1) * HEAD_DIM]
        v_h = v[:, kv * HEAD_DIM : (kv + 1) * HEAD_DIM]
        scores = mask_of(h, mm(q_h, k_h, (1, 1)))
        top = jnp.max(scores, axis=-1, keepdims=True)
        weights = jnp.exp(scores - top)
        probs = (weights / jnp.sum(weights, axis=-1, keepdims=True)).astype(BF16)
        probs_ref[h] = probs
        out_ref[:, h * HEAD_DIM : (h + 1) * HEAD_DIM] = mm(probs, v_h, (1, 0)).astype(BF16)


def self_forward_body(lengths_ref, q_ref, k_ref, v_ref, table_ref, out_ref, probs_ref, bias_ref):
    pair, seq = pl.program_id(0), pl.program_id(1)
    rows, keys = q_ref.shape[0], k_ref.shape[0]
    heads = 2 * GROUPS

    @pl.when(seq == 0)
    def _():
        for h in range(heads):
            line = jnp.broadcast_to(table_ref[h : h + 1, :], (rows, keys))
            bias_ref[h] = pltpu.roll(line, 0, 1, stride=1, stride_axis=0)

    length = lengths_ref[seq]
    i = lax.broadcasted_iota(jnp.int32, (rows, keys), 0)
    j = lax.broadcasted_iota(jnp.int32, (rows, keys), 1)
    allowed = (j <= i) & (j < length)

    def mask_of(h, raw):
        return jnp.where(allowed, raw + bias_ref[h], NEGATIVE)

    softmax_mix(
        q_ref[...] * jnp.asarray(HEAD_DIM**-0.5, BF16),
        k_ref[...],
        v_ref[...],
        heads,
        mask_of,
        probs_ref,
        out_ref,
    )


def cross_forward_body(lengths_ref, q_ref, k_ref, v_ref, segments_ref, out_ref, probs_ref):
    seq = pl.program_id(1)
    rows, keys = q_ref.shape[0], k_ref.shape[0]
    i = lax.broadcasted_iota(jnp.int32, (rows, 1), 0)
    allowed = segments_ref[...] * lengths_ref[seq] <= i * ENC_SEGS

    def mask_of(h, raw):
        return jnp.where(allowed, raw, NEGATIVE)

    softmax_mix(
        q_ref[...] * jnp.asarray(HEAD_DIM**-0.5, BF16),
        k_ref[...],
        v_ref[...],
        2 * GROUPS,
        mask_of,
        probs_ref,
        out_ref,
    )


def attend_forward(queries, keyvals, lengths, extra, kind):
    seqs = lengths.shape[0]
    rows, keys = queries.shape[0] // seqs, keyvals.shape[0] // seqs
    heads = 2 * GROUPS
    if kind == "self":
        extra_spec = pl.BlockSpec((None, heads, keys), lambda p, s, ref: (p, 0, 0))
        extra = extra.reshape(PAIRS, heads, keys)
        scratch = [pltpu.VMEM((heads, rows, keys), F32)]
        body = self_forward_body
    else:
        extra_spec = pl.BlockSpec((None, 1, keys), lambda p, s, ref: (s, 0, 0))
        extra = extra.reshape(seqs, 1, keys)
        scratch = []
        body = cross_forward_body
    return pl.pallas_call(
        body,
        out_shape=[
            jax.ShapeDtypeStruct(queries.shape, BF16),
            jax.ShapeDtypeStruct((seqs, HEADS, rows, keys), BF16),
        ],
        grid_spec=pltpu.PrefetchScalarGridSpec(
            num_scalar_prefetch=1,
            grid=(PAIRS, seqs),
            in_specs=[
                pl.BlockSpec((rows, WIDE), lambda p, s, ref: (s, p)),
                pl.BlockSpec((keys, NARROW), lambda p, s, ref: (s, p)),
                pl.BlockSpec((keys, NARROW), lambda p, s, ref: (s, PAIRS + p)),
                extra_spec,
            ],
            out_specs=[
                pl.BlockSpec((rows, WIDE), lambda p, s, ref: (s, p)),
                pl.BlockSpec((None, heads, rows, keys), lambda p, s, ref: (s, p, 0, 0)),
            ],
            scratch_shapes=scratch,
        ),
        name=kind + "_forward",
    )(lengths, queries, keyvals, keyvals, extra)


def attend_backward_body(with_bias, g_ref, q_ref, k_ref, v_ref, probs_ref, *refs):
    if with_bias:
        dq_ref, dk_ref, dv_ref, diagonal_ref, sums_ref = refs
    else:
        dq_ref, dk_ref, dv_ref = refs
    rows, keys = q_ref.shape[0], k_ref.shape[0]
    heads = 2 * GROUPS
    scale = jnp.asarray(HEAD_DIM**-0.5, BF16)
    g, k, v = g_ref[...], k_ref[...] * scale, v_ref[...]
    q_t, g_t = (q_ref[...] * scale).T, g.T
    dk, dv = [None, None], [None, None]
    for h in range(heads):
        kv = h // GROUPS
        own = slice(h * HEAD_DIM, (h + 1) * HEAD_DIM)
        shared = slice(kv * HEAD_DIM, (kv + 1) * HEAD_DIM)
        probs = probs_ref[h]
        grad_probs = mm(g[:, own], v[:, shared], (1, 1))
        weighted = probs.astype(F32) * grad_probs
        total = jnp.sum(weighted, axis=-1, keepdims=True)
        scores = (weighted - probs.astype(F32) * total).astype(BF16)
        dq_ref[:, own] = mm(scores, k[:, shared], (1, 0)).astype(BF16)
        dk_h = mm(q_t[own], scores, (1, 0))
        dv_h = mm(g_t[own], probs, (1, 0))
        dk[kv] = dk_h if dk[kv] is None else dk[kv] + dk_h
        dv[kv] = dv_h if dv[kv] is None else dv[kv] + dv_h
        if with_bias:
            seq = pl.program_id(1)

            @pl.when(seq == 0)
            def _():
                sums_ref[h] = scores.astype(F32)

            @pl.when(seq != 0)
            def _():
                sums_ref[h] = sums_ref[h] + scores.astype(F32)

    dk_ref[...] = jnp.concatenate(dk, axis=0).T.astype(BF16)
    dv_ref[...] = jnp.concatenate(dv, axis=0).T.astype(BF16)
    if with_bias:

        @pl.when(pl.program_id(1) == pl.num_programs(1) - 1)
        def _():
            step = 8
            for h in range(heads):
                folded = sums_ref[h, :step, :]
                for a in range(1, rows // step):
                    tile = sums_ref[h, a * step : (a + 1) * step, :]
                    folded = folded + pltpu.roll(tile, keys - a * step, 1)
                line = folded[0:1]
                for b in range(1, step):
                    line = line + pltpu.roll(folded, keys - b, 1)[b : b + 1]
                diagonal_ref[h : h + 1, :] = line


def attend_backward(grad_mixed, queries, keyvals, probs, seqs, kind):
    rows, keys = queries.shape[0] // seqs, keyvals.shape[0] // seqs
    heads = 2 * GROUPS
    half = jax.ShapeDtypeStruct((keyvals.shape[0], keyvals.shape[1] // 2), BF16)
    outs = [jax.ShapeDtypeStruct(queries.shape, BF16), half, half]
    out_specs = [
        pl.BlockSpec((rows, WIDE), lambda p, s: (s, p)),
        pl.BlockSpec((keys, NARROW), lambda p, s: (s, p)),
        pl.BlockSpec((keys, NARROW), lambda p, s: (s, p)),
    ]
    scratch = []
    with_bias = kind == "self"
    if with_bias:
        outs.append(jax.ShapeDtypeStruct((PAIRS, heads, keys), F32))
        out_specs.append(pl.BlockSpec((None, heads, keys), lambda p, s: (p, 0, 0)))
        scratch = [pltpu.VMEM((heads, rows, keys), F32)]
    result = pl.pallas_call(
        lambda *refs: attend_backward_body(with_bias, *refs),
        out_shape=outs,
        grid=(PAIRS, seqs),
        in_specs=[
            pl.BlockSpec((rows, WIDE), lambda p, s: (s, p)),
            pl.BlockSpec((rows, WIDE), lambda p, s: (s, p)),
            pl.BlockSpec((keys, NARROW), lambda p, s: (s, p)),
            pl.BlockSpec((keys, NARROW), lambda p, s: (s, PAIRS + p)),
            pl.BlockSpec((None, heads, rows, keys), lambda p, s: (s, p, 0, 0)),
        ],
        out_specs=out_specs,
        scratch_shapes=scratch,
        name=kind + "_backward",
    )(grad_mixed, queries, keyvals, keyvals, probs)
    grad_keyval = jnp.concatenate([result[1], result[2]], axis=1)
    return result[0], grad_keyval, (result[3].reshape(HEADS, keys) if with_bias else None)


def rms_parts(values):
    inv_root = lax.rsqrt(jnp.mean(values * values, axis=-1, keepdims=True) + EPSILON)
    return (values * inv_root, inv_root)


def rms_back(grad_normed, values, inv_root, gain_vec):
    unit_rows = values * inv_root
    grad_unit = grad_normed * gain_vec
    grad_values = inv_root * (
        grad_unit - unit_rows * jnp.mean(grad_unit * unit_rows, axis=-1, keepdims=True)
    )
    return (grad_values, jnp.sum(grad_normed * unit_rows, axis=0))


def gelu_tanh(values):
    return jax.nn.gelu(values, approximate=True)


def per_device(
    tokens,
    encoded,
    cotangent,
    lengths,
    enc_segments,
    placement,
    buckets,
    self_query,
    self_keyval,
    self_out,
    cross_query,
    cross_keyval,
    cross_out,
    feed_in,
    feed_out,
    norm_self,
    norm_cross,
    norm_feed,
    bias_table,
):
    grid = Grid()
    index = grid_index(grid)
    slots, seq_len, width = tokens.shape
    shard = self_query.shape[0]
    devices = 2 * grid.lines * grid.planes
    device = lax.axis_index(AXES)
    group_width = slots * grid.planes
    group_base = device // grid.planes * group_width
    group_order = lax.dynamic_slice_in_dim(placement, group_base, group_width)
    own = device * slots + jnp.arange(slots, dtype=jnp.int32)
    found = jnp.sum(
        jnp.where(
            group_order[None, :] == own[:, None],
            jnp.arange(group_width, dtype=jnp.int32)[None, :],
            0,
        ),
        axis=1,
    ).astype(jnp.int32)
    own_lengths = lax.dynamic_slice_in_dim(lengths, device * slots, slots)
    own_segments = lax.dynamic_slice_in_dim(enc_segments, device * slots, slots)

    tail = bias_table.shape[0]
    columns = [norm_self, norm_cross, norm_feed, jnp.pad(bias_table, (0, shard - tail))]
    small = jnp.pad(jnp.stack(columns, axis=1), ((0, 0), (0, SMALL - len(columns))))
    wide = self_query.shape[1]
    query_self_w, keyval_self_w, smalls = gather_rows(
        grid, index, jnp.concatenate([self_query, self_keyval, small], 1), [wide, wide, SMALL], "first"
    )
    keyval_cross_w, out_self_w = gather_rows(
        grid, index, jnp.concatenate([cross_keyval, self_out], 1), [wide, wide], "second"
    )
    query_cross_w, out_cross_w = gather_rows(
        grid, index, jnp.concatenate([cross_query, cross_out], 1), [wide, wide], "third"
    )
    (feed_in_w,) = gather_rows(grid, index, feed_in, [feed_in.shape[1]], "feed_in")
    (feed_out_w,) = gather_rows(grid, index, feed_out, [feed_out.shape[1]], "feed_out")
    dealt = fetch_dealt(grid, cotangent, found)

    smalls = smalls.astype(F32)
    gain_self, gain_cross, gain_feed = smalls[:, 0], smalls[:, 1], smalls[:, 2]
    table = smalls.reshape(devices, shard, SMALL)[:, :tail, 3].reshape(BUCKETS, HEADS)
    turned = jnp.roll(buckets[::-1], 1)
    hot = (turned[None, :] == jnp.arange(BUCKETS, dtype=jnp.int32)[:, None]).astype(F32)
    table_lines = lax.dot_general(
        table, hot, (((0,), (0,)), ((), ())), precision=lax.Precision.HIGHEST
    )

    hidden_zero = tokens.reshape(slots * seq_len, width).astype(F32)
    unit, root_one = rms_parts(hidden_zero)
    normed_self = (unit * gain_self).astype(BF16)
    queries_self = matmul(normed_self, query_self_w).astype(BF16)
    keyval_self = matmul(normed_self, keyval_self_w).astype(BF16)
    mixed_self, probs_self = attend_forward(
        queries_self, keyval_self, own_lengths, table_lines, "self"
    )
    hidden_one = hidden_zero + matmul(mixed_self, out_self_w)
    unit, root_two = rms_parts(hidden_one)
    normed_cross = (unit * gain_cross).astype(BF16)
    encoded_rows = encoded.reshape(-1, width)
    keyval_cross = matmul(encoded_rows, keyval_cross_w).astype(BF16)
    queries_cross = matmul(normed_cross, query_cross_w).astype(BF16)
    mixed_cross, probs_cross = attend_forward(
        queries_cross, keyval_cross, own_lengths, own_segments, "cross"
    )
    hidden_two = hidden_one + matmul(mixed_cross, out_cross_w)
    unit, root_three = rms_parts(hidden_two)
    normed_feed = (unit * gain_feed).astype(BF16)
    gate_up = matmul(normed_feed, feed_in_w).astype(BF16)
    gate, up = gate_up[:, :FF].astype(F32), gate_up[:, FF:].astype(F32)
    inner = (gelu_tanh(gate) * up).astype(BF16)
    places = jnp.arange(seq_len, dtype=jnp.int32)
    is_valid = (places[None, :] < own_lengths[:, None]).reshape(-1, 1)
    result = hidden_two + matmul(inner, feed_out_w)
    output = jnp.where(is_valid, result, 0.0).astype(BF16).reshape(tokens.shape)

    grad_out = jnp.where(is_valid, dealt.reshape(slots * seq_len, width), jnp.zeros((), BF16))
    grad_feed_out = scatter_rows(grid, matmul_tn(inner, grad_out).astype(BF16))
    grad_inner = matmul_nt(grad_out, feed_out_w)
    activated, gelu_pull = jax.vjp(gelu_tanh, gate)
    grad_gate = gelu_pull(grad_inner * up)[0]
    grad_gate_up = jnp.concatenate([grad_gate.astype(BF16), (grad_inner * activated).astype(BF16)], 1)
    grad_feed_in = scatter_rows(grid, matmul_tn(normed_feed, grad_gate_up).astype(BF16))
    grad_normed = matmul_nt(grad_gate_up, feed_in_w)
    through, grad_gain_feed = rms_back(grad_normed, hidden_two, root_three, gain_feed)
    grad_two = grad_out.astype(F32) + through

    branch = grad_two.astype(BF16)
    grad_cross_out = scatter_rows(grid, matmul_tn(mixed_cross, branch).astype(BF16))
    grad_mixed = matmul_nt(branch, out_cross_w).astype(BF16)
    grad_queries, grad_keyval, _ = attend_backward(
        grad_mixed, queries_cross, keyval_cross, probs_cross, slots, "cross"
    )
    grad_cross = scatter_rows(
        grid,
        jnp.concatenate(
            [
                matmul_tn(normed_cross, grad_queries).astype(BF16),
                matmul_tn(encoded_rows, grad_keyval).astype(BF16),
            ],
            1,
        ),
    )
    grad_encoded = matmul_nt(grad_keyval, keyval_cross_w).reshape(encoded.shape)
    grad_normed = matmul_nt(grad_queries, query_cross_w)
    through, grad_gain_cross = rms_back(grad_normed, hidden_one, root_two, gain_cross)
    grad_one = grad_two + through

    branch = grad_one.astype(BF16)
    grad_self_out = scatter_rows(grid, matmul_tn(mixed_self, branch).astype(BF16))
    grad_mixed = matmul_nt(branch, out_self_w).astype(BF16)
    grad_queries, grad_keyval, diagonals = attend_backward(
        grad_mixed, queries_self, keyval_self, probs_self, slots, "self"
    )
    grad_table = lax.dot_general(
        hot, diagonals, (((1,), (1,)), ((), ())), precision=lax.Precision.HIGHEST
    )
    grad_normed = matmul_nt(grad_queries, query_self_w) + matmul_nt(grad_keyval, keyval_self_w)
    through, grad_gain_self = rms_back(grad_normed, hidden_zero, root_one, gain_self)
    grad_tokens = (grad_one + through).reshape(tokens.shape)
    table_rows = jnp.pad(grad_table.reshape(devices, tail), ((0, 0), (0, shard - tail))).reshape(-1)
    columns = [grad_gain_self, grad_gain_cross, grad_gain_feed, table_rows]
    small = jnp.pad(jnp.stack(columns, axis=1), ((0, 0), (0, SMALL - len(columns)))).astype(BF16)
    grad_self = scatter_rows(
        grid,
        jnp.concatenate(
            [
                matmul_tn(normed_self, grad_queries).astype(BF16),
                matmul_tn(normed_self, grad_keyval).astype(BF16),
                small,
            ],
            1,
        ),
    )
    return (
        output,
        grad_tokens,
        grad_encoded,
        grad_self[:, :wide],
        grad_self[:, wide : 2 * wide],
        grad_self_out,
        grad_cross[:, :wide],
        grad_cross[:, wide:],
        grad_cross_out,
        grad_feed_in,
        grad_feed_out,
        grad_self[:, 2 * wide],
        grad_self[:, 2 * wide + 1],
        grad_self[:, 2 * wide + 2],
        grad_self[:tail, 2 * wide + 3],
    )


def solution(mesh):
    whole = P(AXES, None, None)
    rows, flat = P(AXES, None), P(AXES)
    return jax.shard_map(
        per_device,
        mesh=mesh,
        in_specs=(whole,) * 3 + (P(),) * 4 + (rows,) * 8 + (flat,) * 4,
        out_specs=(whole,) * 3 + (rows,) * 8 + (flat,) * 4,
        check_vma=False,
    )
```

```python
import math

import jax
import jax.numpy as jnp
from jax import lax
from jax.experimental import pallas as pl
from jax.experimental.pallas import tpu as pltpu
from jax.sharding import PartitionSpec as P

HEADS = 16
HEAD_DIM = 64
KV_HEADS = 8
FF = 2816
BUCKETS = 32
ENC_SEGS = 4

EPSILON = 1e-06
NEGATIVE = -1e30
AXES = ("dp", "fsdp")
BF16 = jnp.bfloat16
F32 = jnp.float32
SMALL = 128


def matmul(left_op, right_op):
    return jnp.dot(left_op, right_op, preferred_element_type=F32)


def matmul_tn(left_op, right_op):
    return lax.dot_general(left_op, right_op, (((0,), (0,)), ((), ())), preferred_element_type=F32)


def matmul_nt(left_op, right_op):
    return lax.dot_general(left_op, right_op, (((1,), (1,)), ((), ())), preferred_element_type=F32)


class Grid:
    def __init__(self):
        self.planes = lax.axis_size("fsdp")
        self.lines = lax.axis_size("dp") // 2
        dp = lax.axis_index("dp")
        self.line, self.core, self.plane = dp // 2, dp % 2, lax.axis_index("fsdp")

    def send(self, array, line=0, core=0, plane=0):
        pairs = []
        for source in range(2 * self.lines * self.planes):
            z, c, s = source // (2 * self.planes), source // self.planes % 2, source % self.planes
            pairs.append((source, ((z ^ line) * 2 + (c ^ core)) * self.planes + (s ^ plane)))
        return lax.ppermute(array, AXES, pairs)


def line_groups(grid):
    return [
        [(z * 2 + c) * grid.planes + s for z in range(grid.lines)]
        for c in range(2)
        for s in range(grid.planes)
    ]


def spread(grid, block):
    if grid.planes != 4:
        return [(0, None, block)] + [
            (j, None, grid.send(block, plane=j)) for j in range(1, grid.planes)
        ]
    half = block.shape[0] // 2
    by_x = grid.send(block, plane=1)
    by_y = grid.send(block, plane=2)
    low = grid.send(by_x[:half], plane=2)
    high = grid.send(by_y[half:], plane=1)
    return [(0, None, block), (1, None, by_x), (2, None, by_y), (3, 0, low), (3, 1, high)]


def gather_rows(grid, index, shard, widths, name):
    rows, width = shard.shape
    lines, planes = grid.lines, grid.planes
    half = lines // 2
    block = lax.all_gather(shard, AXES, axis=0, axis_index_groups=line_groups(grid))
    pieces = spread(grid, block)
    both = [(0, *piece) for piece in pieces] + [
        (1, j, part, grid.send(array, core=1)) for j, part, array in pieces
    ]
    order = [(c, j) for c in range(2) for j in range(planes)]
    n_in = len(both)

    def in_map(source):
        c, j, part, _ = both[source]
        turn = order.index((c, j))

        def index_map(h, p, ref):
            at = jnp.where(p < turn, jnp.maximum(h - 1, 0), h) if part is None else 0
            return (at, 0, 0)

        return index_map

    def out_map(h, p, ref):
        return (h, ref[1] ^ (p // planes), ref[2] ^ (p % planes), 0, 0)

    def body(index_ref, *refs):
        ins, outs = refs[:n_in], refs[n_in:]
        h, p = pl.program_id(0), pl.program_id(1)
        for source, (c, j, part, _) in enumerate(both):
            hit = p == order.index((c, j))
            if part is not None:
                hit = hit & (h == part)

            @pl.when(hit)
            def _(source=source):
                offset = 0
                for out, w in zip(outs, widths):
                    out[...] = ins[source][:, :, offset : offset + w].reshape(out.shape)
                    offset += w

    whole = pl.pallas_call(
        body,
        out_shape=[
            jax.ShapeDtypeStruct((lines, 2, planes, rows, w), shard.dtype) for w in widths
        ],
        grid_spec=pltpu.PrefetchScalarGridSpec(
            num_scalar_prefetch=1,
            grid=(2, len(order)),
            in_specs=[pl.BlockSpec((half, rows, width), in_map(i)) for i in range(n_in)],
            out_specs=[pl.BlockSpec((half, 1, 1, rows, w), out_map) for w in widths],
        ),
        name=name,
    )(index, *[array for _, _, _, array in both])
    return [array.reshape(-1, array.shape[-1]) for array in whole]


def core_columns(grid, array, core):
    tokens = array.shape[0]
    split = array.reshape(tokens, grid.lines, 2, -1)
    return lax.dynamic_index_in_dim(split, core, 2, keepdims=False).reshape(tokens, -1)


def weight_grad(grid, pairs, extra=None):
    other, mine = [], []
    for left, right in pairs:
        other.append(matmul_tn(core_columns(grid, left, 1 - grid.core), right))
        mine.append(matmul_tn(core_columns(grid, left, grid.core), right))
    if extra is not None:
        split = extra.reshape(grid.lines, 2, -1, extra.shape[1])
        for core, terms in ((1 - grid.core, other), (grid.core, mine)):
            rows = lax.dynamic_index_in_dim(split, core, 1, keepdims=False)
            terms.append(rows.reshape(-1, extra.shape[1]))
    other = jnp.concatenate([t.astype(BF16) for t in other], 1)
    other = grid.send(other, core=1)
    offset, sums = 0, []
    for term in mine:
        add = other[:, offset : offset + term.shape[1]]
        sums.append((term + add.astype(F32)).astype(BF16))
        offset += term.shape[1]
    return jnp.concatenate(sums, 1)


def scatter_rows(grid, terms):
    lines, planes = grid.lines, grid.planes
    width = terms.shape[-1]
    terms = terms.reshape(lines, planes, -1, width)

    def block(j, span=slice(None)):
        return lax.dynamic_index_in_dim(terms[span], grid.plane ^ j, 1, keepdims=False).astype(F32)

    if planes != 4:
        own = block(0)
        for j in range(1, planes):
            own = own + grid.send(block(j).astype(BF16), plane=j).astype(F32)
    else:
        half = lines // 2
        low = grid.send(block(3, slice(0, half)).astype(BF16), plane=2).astype(F32)
        high = grid.send(block(3, slice(half, lines)).astype(BF16), plane=1).astype(F32)
        by_x, by_y = block(1), block(2)
        by_x = jnp.concatenate([by_x[:half] + low, by_x[half:]]).astype(BF16)
        by_y = jnp.concatenate([by_y[:half], by_y[half:] + high]).astype(BF16)
        own = block(0) + grid.send(by_x, plane=1).astype(F32)
        own = own + grid.send(by_y, plane=2).astype(F32)
    total = lax.psum_scatter(
        own.astype(BF16), AXES, scatter_dimension=0, axis_index_groups=line_groups(grid)
    )
    return total.astype(F32)


def fetch_dealt(grid, array, found):
    slots = array.shape[0]
    pieces = spread(grid, array)
    half = slots // 2
    rows = []
    for t in range(slots):
        away, slot = found[t] // slots ^ grid.plane, found[t] % slots
        row = jnp.zeros(array.shape[1:], array.dtype)
        for j, part, piece in pieces:
            for k in range(piece.shape[0]):
                at = k if part is None else part * half + k
                row = jnp.where((away == j) & (slot == at), piece[k], row)
        rows.append(row)
    return jnp.stack(rows)


def tie(*arrays):
    return lax.optimization_barrier(arrays)


def grid_index(grid):
    return jnp.stack([grid.line, grid.core, grid.plane]).astype(jnp.int32)


PAIRS = KV_HEADS // 2
GROUPS = HEADS // KV_HEADS
WIDE = 2 * GROUPS * HEAD_DIM
NARROW = 2 * HEAD_DIM


def mm(left, right, dims):
    return lax.dot_general(left, right, ((dims[:1], dims[1:]), ((), ())), preferred_element_type=F32)


def softmax_mix(q, k, v, heads, mask_of, probs_ref, out_ref):
    for h in range(heads):
        kv = h // GROUPS
        q_h = q[:, h * HEAD_DIM : (h + 1) * HEAD_DIM]
        k_h = k[:, kv * HEAD_DIM : (kv + 1) * HEAD_DIM]
        v_h = v[:, kv * HEAD_DIM : (kv + 1) * HEAD_DIM]
        scores = mask_of(h, mm(q_h, k_h, (1, 1)))
        top = jnp.max(scores, axis=-1, keepdims=True)
        weights = jnp.exp(scores - top)
        probs = (weights / jnp.sum(weights, axis=-1, keepdims=True)).astype(BF16)
        probs_ref[h] = probs
        out_ref[:, h * HEAD_DIM : (h + 1) * HEAD_DIM] = mm(probs, v_h, (1, 0)).astype(BF16)


def self_forward_body(lengths_ref, q_ref, k_ref, v_ref, table_ref, out_ref, probs_ref, bias_ref):
    pair, seq = pl.program_id(0), pl.program_id(1)
    rows, keys = q_ref.shape[0], k_ref.shape[0]
    heads = 2 * GROUPS

    @pl.when(seq == 0)
    def _():
        for h in range(heads):
            line = jnp.broadcast_to(table_ref[h : h + 1, :], (rows, keys))
            bias_ref[h] = pltpu.roll(line, 0, 1, stride=1, stride_axis=0)

    length = lengths_ref[seq]
    i = lax.broadcasted_iota(jnp.int32, (rows, keys), 0)
    j = lax.broadcasted_iota(jnp.int32, (rows, keys), 1)
    allowed = (j <= i) & (j < length)

    def mask_of(h, raw):
        return jnp.where(allowed, raw + bias_ref[h], NEGATIVE)

    softmax_mix(
        q_ref[...] * jnp.asarray(HEAD_DIM**-0.5, BF16),
        k_ref[...],
        v_ref[...],
        heads,
        mask_of,
        probs_ref,
        out_ref,
    )


def cross_forward_body(lengths_ref, q_ref, k_ref, v_ref, segments_ref, out_ref, probs_ref):
    seq = pl.program_id(1)
    rows, keys = q_ref.shape[0], k_ref.shape[0]
    i = lax.broadcasted_iota(jnp.int32, (rows, 1), 0)
    allowed = segments_ref[...] * lengths_ref[seq] <= i * ENC_SEGS

    def mask_of(h, raw):
        return jnp.where(allowed, raw, NEGATIVE)

    softmax_mix(
        q_ref[...] * jnp.asarray(HEAD_DIM**-0.5, BF16),
        k_ref[...],
        v_ref[...],
        2 * GROUPS,
        mask_of,
        probs_ref,
        out_ref,
    )


def attend_forward(queries, keyvals, lengths, extra, kind):
    seqs = lengths.shape[0]
    rows, keys = queries.shape[0] // seqs, keyvals.shape[0] // seqs
    heads = 2 * GROUPS
    if kind == "self":
        extra_spec = pl.BlockSpec((None, heads, keys), lambda p, s, ref: (p, 0, 0))
        extra = extra.reshape(PAIRS, heads, keys)
        scratch = [pltpu.VMEM((heads, rows, keys), F32)]
        body = self_forward_body
    else:
        extra_spec = pl.BlockSpec((None, 1, keys), lambda p, s, ref: (s, 0, 0))
        extra = extra.reshape(seqs, 1, keys)
        scratch = []
        body = cross_forward_body
    return pl.pallas_call(
        body,
        out_shape=[
            jax.ShapeDtypeStruct(queries.shape, BF16),
            jax.ShapeDtypeStruct((seqs, HEADS, rows, keys), BF16),
        ],
        grid_spec=pltpu.PrefetchScalarGridSpec(
            num_scalar_prefetch=1,
            grid=(PAIRS, seqs),
            in_specs=[
                pl.BlockSpec((rows, WIDE), lambda p, s, ref: (s, p)),
                pl.BlockSpec((keys, NARROW), lambda p, s, ref: (s, p)),
                pl.BlockSpec((keys, NARROW), lambda p, s, ref: (s, PAIRS + p)),
                extra_spec,
            ],
            out_specs=[
                pl.BlockSpec((rows, WIDE), lambda p, s, ref: (s, p)),
                pl.BlockSpec((None, heads, rows, keys), lambda p, s, ref: (s, p, 0, 0)),
            ],
            scratch_shapes=scratch,
        ),
        name=kind + "_forward",
    )(lengths, queries, keyvals, keyvals, extra)


def attend_backward_body(with_bias, g_ref, q_ref, k_ref, v_ref, probs_ref, *refs):
    if with_bias:
        dq_ref, dk_ref, dv_ref, diagonal_ref, sums_ref = refs
    else:
        dq_ref, dk_ref, dv_ref = refs
    rows, keys = q_ref.shape[0], k_ref.shape[0]
    heads = 2 * GROUPS
    scale = jnp.asarray(HEAD_DIM**-0.5, BF16)
    g, k, v = g_ref[...], k_ref[...] * scale, v_ref[...]
    q_t, g_t = (q_ref[...] * scale).T, g.T
    dk, dv = [None, None], [None, None]
    for h in range(heads):
        kv = h // GROUPS
        own = slice(h * HEAD_DIM, (h + 1) * HEAD_DIM)
        shared = slice(kv * HEAD_DIM, (kv + 1) * HEAD_DIM)
        probs = probs_ref[h]
        grad_probs = mm(g[:, own], v[:, shared], (1, 1))
        weighted = probs.astype(F32) * grad_probs
        total = jnp.sum(weighted, axis=-1, keepdims=True)
        scores = (weighted - probs.astype(F32) * total).astype(BF16)
        dq_ref[:, own] = mm(scores, k[:, shared], (1, 0)).astype(BF16)
        dk_h = mm(q_t[own], scores, (1, 0))
        dv_h = mm(g_t[own], probs, (1, 0))
        dk[kv] = dk_h if dk[kv] is None else dk[kv] + dk_h
        dv[kv] = dv_h if dv[kv] is None else dv[kv] + dv_h
        if with_bias:
            seq = pl.program_id(1)

            @pl.when(seq == 0)
            def _():
                sums_ref[h] = scores.astype(F32)

            @pl.when(seq != 0)
            def _():
                sums_ref[h] = sums_ref[h] + scores.astype(F32)

    dk_ref[...] = jnp.concatenate(dk, axis=0).T.astype(BF16)
    dv_ref[...] = jnp.concatenate(dv, axis=0).T.astype(BF16)
    if with_bias:

        @pl.when(pl.program_id(1) == pl.num_programs(1) - 1)
        def _():
            step = 8
            for h in range(heads):
                folded = sums_ref[h, :step, :]
                for a in range(1, rows // step):
                    tile = sums_ref[h, a * step : (a + 1) * step, :]
                    folded = folded + pltpu.roll(tile, keys - a * step, 1)
                line = folded[0:1]
                for b in range(1, step):
                    line = line + pltpu.roll(folded, keys - b, 1)[b : b + 1]
                diagonal_ref[h : h + 1, :] = line


def attend_backward(grad_mixed, queries, keyvals, probs, seqs, kind):
    rows, keys = queries.shape[0] // seqs, keyvals.shape[0] // seqs
    heads = 2 * GROUPS
    half = jax.ShapeDtypeStruct((keyvals.shape[0], keyvals.shape[1] // 2), BF16)
    outs = [jax.ShapeDtypeStruct(queries.shape, BF16), half, half]
    out_specs = [
        pl.BlockSpec((rows, WIDE), lambda p, s: (s, p)),
        pl.BlockSpec((keys, NARROW), lambda p, s: (s, p)),
        pl.BlockSpec((keys, NARROW), lambda p, s: (s, p)),
    ]
    scratch = []
    with_bias = kind == "self"
    if with_bias:
        outs.append(jax.ShapeDtypeStruct((PAIRS, heads, keys), F32))
        out_specs.append(pl.BlockSpec((None, heads, keys), lambda p, s: (p, 0, 0)))
        scratch = [pltpu.VMEM((heads, rows, keys), F32)]
    result = pl.pallas_call(
        lambda *refs: attend_backward_body(with_bias, *refs),
        out_shape=outs,
        grid=(PAIRS, seqs),
        in_specs=[
            pl.BlockSpec((rows, WIDE), lambda p, s: (s, p)),
            pl.BlockSpec((rows, WIDE), lambda p, s: (s, p)),
            pl.BlockSpec((keys, NARROW), lambda p, s: (s, p)),
            pl.BlockSpec((keys, NARROW), lambda p, s: (s, PAIRS + p)),
            pl.BlockSpec((None, heads, rows, keys), lambda p, s: (s, p, 0, 0)),
        ],
        out_specs=out_specs,
        scratch_shapes=scratch,
        name=kind + "_backward",
    )(grad_mixed, queries, keyvals, keyvals, probs)
    grad_keyval = jnp.concatenate([result[1], result[2]], axis=1)
    return result[0], grad_keyval, (result[3].reshape(HEADS, keys) if with_bias else None)


def rms_parts(values):
    inv_root = lax.rsqrt(jnp.mean(values * values, axis=-1, keepdims=True) + EPSILON)
    return (values * inv_root, inv_root)


def rms_back(grad_normed, values, inv_root, gain_vec):
    unit_rows = values * inv_root
    grad_unit = grad_normed * gain_vec
    grad_values = inv_root * (
        grad_unit - unit_rows * jnp.mean(grad_unit * unit_rows, axis=-1, keepdims=True)
    )
    return (grad_values, jnp.sum(grad_normed * unit_rows, axis=0))


def gelu_tanh(values):
    return jax.nn.gelu(values, approximate=True)


def per_device(
    tokens,
    encoded,
    cotangent,
    lengths,
    enc_segments,
    placement,
    buckets,
    self_query,
    self_keyval,
    self_out,
    cross_query,
    cross_keyval,
    cross_out,
    feed_in,
    feed_out,
    norm_self,
    norm_cross,
    norm_feed,
    bias_table,
):
    grid = Grid()
    index = grid_index(grid)
    slots, seq_len, width = tokens.shape
    shard = self_query.shape[0]
    devices = 2 * grid.lines * grid.planes
    device = lax.axis_index(AXES)
    group_width = slots * grid.planes
    group_base = device // grid.planes * group_width
    group_order = lax.dynamic_slice_in_dim(placement, group_base, group_width)
    own = device * slots + jnp.arange(slots, dtype=jnp.int32)
    found = jnp.sum(
        jnp.where(
            group_order[None, :] == own[:, None],
            jnp.arange(group_width, dtype=jnp.int32)[None, :],
            0,
        ),
        axis=1,
    ).astype(jnp.int32)
    own_lengths = lax.dynamic_slice_in_dim(lengths, device * slots, slots)
    own_segments = lax.dynamic_slice_in_dim(enc_segments, device * slots, slots)

    tail = bias_table.shape[0]
    columns = [norm_self, norm_cross, norm_feed, jnp.pad(bias_table, (0, shard - tail))]
    small = jnp.pad(jnp.stack(columns, axis=1), ((0, 0), (0, SMALL - len(columns))))
    wide = self_query.shape[1]
    query_self_w, keyval_self_w, smalls = gather_rows(
        grid, index, jnp.concatenate([self_query, self_keyval, small], 1), [wide, wide, SMALL], "first"
    )
    keyval_cross_w, out_self_w = gather_rows(
        grid, index, jnp.concatenate([cross_keyval, self_out], 1), [wide, wide], "second"
    )
    query_cross_w, out_cross_w = gather_rows(
        grid, index, jnp.concatenate([cross_query, cross_out], 1), [wide, wide], "third"
    )
    (feed_in_w,) = gather_rows(grid, index, feed_in, [feed_in.shape[1]], "feed_in")
    (feed_out_w,) = gather_rows(grid, index, feed_out, [feed_out.shape[1]], "feed_out")
    dealt = fetch_dealt(grid, cotangent, found)

    smalls = smalls.astype(F32)
    gain_self, gain_cross, gain_feed = smalls[:, 0], smalls[:, 1], smalls[:, 2]
    table = smalls.reshape(devices, shard, SMALL)[:, :tail, 3].reshape(BUCKETS, HEADS)
    turned = jnp.roll(buckets[::-1], 1)
    hot = (turned[None, :] == jnp.arange(BUCKETS, dtype=jnp.int32)[:, None]).astype(F32)
    table_lines = lax.dot_general(
        table, hot, (((0,), (0,)), ((), ())), precision=lax.Precision.HIGHEST
    )

    hidden_zero = tokens.reshape(slots * seq_len, width).astype(F32)
    unit, root_one = rms_parts(hidden_zero)
    normed_self = (unit * gain_self).astype(BF16)
    queries_self = matmul(normed_self, query_self_w).astype(BF16)
    keyval_self = matmul(normed_self, keyval_self_w).astype(BF16)
    mixed_self, probs_self = attend_forward(
        queries_self, keyval_self, own_lengths, table_lines, "self"
    )
    hidden_one = hidden_zero + matmul(mixed_self, out_self_w)
    unit, root_two = rms_parts(hidden_one)
    normed_cross = (unit * gain_cross).astype(BF16)
    encoded_rows = encoded.reshape(-1, width)
    keyval_cross = matmul(encoded_rows, keyval_cross_w).astype(BF16)
    queries_cross = matmul(normed_cross, query_cross_w).astype(BF16)
    mixed_cross, probs_cross = attend_forward(
        queries_cross, keyval_cross, own_lengths, own_segments, "cross"
    )
    hidden_two = hidden_one + matmul(mixed_cross, out_cross_w)
    unit, root_three = rms_parts(hidden_two)
    normed_feed = (unit * gain_feed).astype(BF16)
    gate_up = matmul(normed_feed, feed_in_w).astype(BF16)
    gate, up = gate_up[:, :FF].astype(F32), gate_up[:, FF:].astype(F32)
    inner = (gelu_tanh(gate) * up).astype(BF16)
    places = jnp.arange(seq_len, dtype=jnp.int32)
    is_valid = (places[None, :] < own_lengths[:, None]).reshape(-1, 1)
    result = hidden_two + matmul(inner, feed_out_w)
    output = jnp.where(is_valid, result, 0.0).astype(BF16).reshape(tokens.shape)

    grad_out = jnp.where(is_valid, dealt.reshape(slots * seq_len, width), jnp.zeros((), BF16))
    sum_feed_out = weight_grad(grid, [(inner, grad_out)])
    grad_out, sum_feed_out = tie(grad_out, sum_feed_out)
    grad_feed_out = scatter_rows(grid, sum_feed_out)
    grad_inner = matmul_nt(grad_out, feed_out_w)
    activated, gelu_pull = jax.vjp(gelu_tanh, gate)
    grad_gate = gelu_pull(grad_inner * up)[0]
    grad_gate_up = jnp.concatenate([grad_gate.astype(BF16), (grad_inner * activated).astype(BF16)], 1)
    sum_feed_in = weight_grad(grid, [(normed_feed, grad_gate_up)])
    grad_gate_up, sum_feed_in = tie(grad_gate_up, sum_feed_in)
    grad_feed_in = scatter_rows(grid, sum_feed_in)
    grad_normed = matmul_nt(grad_gate_up, feed_in_w)
    through, grad_gain_feed = rms_back(grad_normed, hidden_two, root_three, gain_feed)
    grad_two = grad_out.astype(F32) + through

    branch = grad_two.astype(BF16)
    grad_mixed = matmul_nt(branch, out_cross_w).astype(BF16)
    grad_queries, grad_keyval, _ = attend_backward(
        grad_mixed, queries_cross, keyval_cross, probs_cross, slots, "cross"
    )
    sum_cross = weight_grad(
        grid, [(normed_cross, grad_queries), (encoded_rows, grad_keyval), (mixed_cross, branch)]
    )
    grad_queries, grad_keyval, sum_cross = tie(grad_queries, grad_keyval, sum_cross)
    grad_cross = scatter_rows(grid, sum_cross)
    grad_encoded = matmul_nt(grad_keyval, keyval_cross_w).reshape(encoded.shape)
    grad_normed = matmul_nt(grad_queries, query_cross_w)
    through, grad_gain_cross = rms_back(grad_normed, hidden_one, root_two, gain_cross)
    grad_one = grad_two + through

    branch = grad_one.astype(BF16)
    grad_mixed = matmul_nt(branch, out_self_w).astype(BF16)
    grad_queries, grad_keyval, diagonals = attend_backward(
        grad_mixed, queries_self, keyval_self, probs_self, slots, "self"
    )
    grad_table = lax.dot_general(
        hot, diagonals, (((1,), (1,)), ((), ())), precision=lax.Precision.HIGHEST
    )
    grad_normed = matmul_nt(grad_queries, query_self_w) + matmul_nt(grad_keyval, keyval_self_w)
    through, grad_gain_self = rms_back(grad_normed, hidden_zero, root_one, gain_self)
    grad_tokens = (grad_one + through).reshape(tokens.shape)
    table_rows = jnp.pad(grad_table.reshape(devices, tail), ((0, 0), (0, shard - tail))).reshape(-1)
    columns = [grad_gain_self, grad_gain_cross, grad_gain_feed, table_rows]
    small = jnp.pad(jnp.stack(columns, axis=1), ((0, 0), (0, SMALL - len(columns))))
    grad_self = scatter_rows(
        grid,
        weight_grad(
            grid,
            [(normed_self, grad_queries), (normed_self, grad_keyval), (mixed_self, branch)],
            small,
        ),
    )
    return (
        output,
        grad_tokens,
        grad_encoded,
        grad_self[:, :wide],
        grad_self[:, wide : 2 * wide],
        grad_self[:, 2 * wide : 3 * wide],
        grad_cross[:, :wide],
        grad_cross[:, wide : 2 * wide],
        grad_cross[:, 2 * wide :],
        grad_feed_in,
        grad_feed_out,
        grad_self[:, 3 * wide],
        grad_self[:, 3 * wide + 1],
        grad_self[:, 3 * wide + 2],
        grad_self[:tail, 3 * wide + 3],
    )


def solution(mesh):
    whole = P(AXES, None, None)
    rows, flat = P(AXES, None), P(AXES)
    return jax.shard_map(
        per_device,
        mesh=mesh,
        in_specs=(whole,) * 3 + (P(),) * 4 + (rows,) * 8 + (flat,) * 4,
        out_specs=(whole,) * 3 + (rows,) * 8 + (flat,) * 4,
        check_vma=False,
    )
```
